32 devices in a mesh: space: 16 (over z, y, x), coil: 2 (over core).
Axes of the slice: x: 2, y: 2, z: 4, core: 2. Of those that a mesh axis runs over, the one named last changes fastest.
Arguments:
- state: bfloat16 [32, 2, 1024, 768], P(None, None, 'space', 'coil'), may hold values from -6 to 6
- sens: float32 [2, 16, 2, 1024, 768], P(None, 'coil', None, 'space'), may hold values from -2 to 2
- kdata: float32 [2, 16, 2, 768, 1024], P(None, 'coil', None, 'space'), may hold values from -3 to 3
- mask: int32 [768, 1024], P('space'), may hold values 0 or 1
- inject: float32 [32, 2], replicated, may hold values from -4 to 4
- kernels: bfloat16 [4, 27, 16, 16], replicated, may hold values from -0.3125 to 0.3125
- biases: float32 [4, 16], replicated, may hold values from -3 to 3
- mixers: bfloat16 [4, 16, 16], replicated, may hold values from -1.5 to 1.5
Outputs:
- new_state: bfloat16 [32, 2, 1024, 768], P(None, None, 'space', 'coil')
- gradient: float32 [2, 2, 1024, 768], P(None, None, 'space', 'coil')
The draws below stay inside these ranges and needn't reach their ends.
All inputs are finite; a program needn't handle non-finite values. No bound on the sum of `mask` on one device may be relied on, other than what follows from the above.
Results may differ from the reference program's by a relative error of at most 0.015.
Values may be sent and summed in bfloat16 or wider, within the bound.
A program may use at most 128 MiB of HBM per device.

```python
import jax
import jax.numpy as jnp
from jax import lax

NPE = 1024
NPAR = 768
COILS = 16
CH = 32
POS = 2
COUPLINGS = 4


def with_ends(result, key, smallest, largest):
    index_at = [jax.random.randint(jax.random.fold_in(key, axis), (), 0, length) for axis, length in enumerate(result.shape)]
    widest = result.shape.index(max(result.shape))
    neighbour = index_at[:widest] + [(index_at[widest] + 1) % result.shape[widest]] + index_at[widest + 1:]
    return result.at[tuple(index_at)].set(smallest).at[tuple(neighbour)].set(largest)


def steps_of(stream_key, dims, cuts, least, largest):
    loudness = 1.0
    for dim, blocks in cuts:
        steps = jax.random.uniform(jax.random.fold_in(jax.random.fold_in(stream_key, 6), dim), (blocks,), jnp.float32, least / len(cuts), largest / len(cuts))
        loudness = loudness * jnp.repeat(jnp.exp(steps), dims[dim] // blocks).reshape((-1,) + (1,) * (len(dims) - 1 - dim))
    return loudness


def normal_values(key, dims, scale, reach, cuts=(), held_as=jnp.bfloat16):
    values = scale * jax.random.normal(key, dims, jnp.float32)
    if cuts:
        values = values * steps_of(key, dims, cuts, -0.22, 0.18)
    return jnp.clip(values, -reach, reach).astype(held_as)


def setup_inputs(seed: int = 0) -> dict:
    key_of = jax.random.split(jax.random.key(seed), 9)
    state = normal_values(key_of[0], (CH, POS, NPE, NPAR), 1.0, 6.0, ((2, 16), (3, 2)))
    sens = normal_values(key_of[1], (2, COILS, POS, NPE, NPAR), 0.25, 2.0, ((1, 2), (3, 16)), jnp.float32)
    kdata = normal_values(key_of[2], (2, COILS, POS, NPAR, NPE), 0.35, 3.0, ((1, 2), (3, 16)), jnp.float32)
    mask = with_ends((jax.random.randint(key_of[3], (NPAR, NPE), 0, 3) < 1).astype(jnp.int32), jax.random.fold_in(key_of[3], 1), 0, 1)
    inject = normal_values(key_of[4], (CH, 2), 2 ** -0.5, 4.0, (), jnp.float32)
    kernels = normal_values(key_of[5], (COUPLINGS, 27, CH // 2, CH // 2), (27 * (CH // 2)) ** -0.5, 0.3125)
    biases = normal_values(key_of[6], (COUPLINGS, CH // 2), 0.5, 3.0, (), jnp.float32)
    mixers = normal_values(key_of[7], (COUPLINGS, CH // 2, CH // 2), (CH // 2) ** -0.5, 1.5)
    return dict(state=state, sens=sens, kdata=kdata, mask=mask, inject=inject, kernels=kernels, biases=biases, mixers=mixers)


def coupling(source, target, kernel, bias, mixer):
    weight = jnp.transpose(kernel.astype(jnp.float32).reshape(3, 3, 3, kernel.shape[1], kernel.shape[2]), (3, 4, 0, 1, 2))
    raw = lax.conv_general_dilated(source.astype(jnp.float32)[None], weight, (1, 1, 1), "SAME", dimension_numbers=("NCDHW", "OIDHW", "NCDHW"), precision=lax.Precision.HIGHEST)[0]
    hidden = jax.nn.relu(raw + bias[:, None, None, None]).astype(jnp.bfloat16)
    mixed = jnp.einsum("oi,ipqr->opqr", mixer.astype(jnp.float32), hidden.astype(jnp.float32), precision=lax.Precision.HIGHEST)
    return (target.astype(jnp.float32) + mixed).astype(jnp.bfloat16)


def reference(state, sens, kdata, mask, inject, kernels, biases, mixers):
    estimate = state[0].astype(jnp.float32) + 1j * state[1].astype(jnp.float32)
    weight = mask.astype(jnp.float32)

    def one_coil(total, pieces):
        sens_real, sens_imag, data_real, data_imag = pieces
        profile = sens_real + 1j * sens_imag
        spectrum = jnp.fft.fft2(profile * estimate, axes=(-2, -1), norm="ortho")
        spectrum = jnp.swapaxes(spectrum, -1, -2)
        residual = weight * (spectrum - (data_real + 1j * data_imag))
        image = jnp.fft.ifft2(jnp.swapaxes(residual, -1, -2), axes=(-2, -1), norm="ortho")
        term = jnp.conj(profile) * image
        return total + jnp.stack([jnp.real(term), jnp.imag(term)]).astype(jnp.float32), None

    start = jnp.zeros((2, POS, NPE, NPAR), jnp.float32)
    gradient, _ = lax.scan(one_coil, start, (sens[0], sens[1], kdata[0], kdata[1]))
    added = jnp.einsum("cg,gpqr->cpqr", inject, gradient, precision=lax.Precision.HIGHEST)
    merged = (state.astype(jnp.float32) + added).astype(jnp.bfloat16)
    half = CH // 2
    first = merged[:half]
    second = merged[half:]
    for layer in range(COUPLINGS):
        if layer % 2 == 0:
            second = coupling(first, second, kernels[layer], biases[layer], mixers[layer])
        else:
            first = coupling(second, first, kernels[layer], biases[layer], mixers[layer])
    new_state = jnp.concatenate([first, second], axis=0)
    return new_state, gradient
```

```python
import functools
import math

import jax
import jax.numpy as jnp
from jax import lax
from jax.experimental import pallas as pl
from jax.experimental.pallas import tpu as pltpu
from jax.sharding import PartitionSpec as P


def dft_table(length):
    index = lax.iota(jnp.int32, length)
    product = index[:, None] * index[None, :] % length
    angle = product.astype(jnp.float32) * (2.0 * math.pi / length)
    scale = 1.0 / math.sqrt(length)
    return jnp.concatenate([jnp.cos(angle) * scale, jnp.sin(angle) * scale], axis=1).astype(jnp.bfloat16)


def transform(stacked, table, length, sign, form):
    result = jnp.einsum(form, stacked.astype(jnp.bfloat16), table, preferred_element_type=jnp.float32)
    real_cos = result[0, ..., :length]
    real_sin = result[0, ..., length:]
    imag_cos = result[1, ..., :length]
    imag_sin = result[1, ..., length:]
    return jnp.stack([real_cos - sign * imag_sin, imag_cos + sign * real_sin])


HALO = 4
BLOCK = 6


def coupling_weights(kernels):
    layers, _, outs, ins = kernels.shape
    taps = kernels.reshape(layers, 3, 3, 3, outs, ins)
    rows = []
    for out_pos in range(2):
        rows.append(jnp.concatenate([taps[:, in_pos - out_pos + 1] for in_pos in range(2)], axis=-1))
    mixed = jnp.concatenate(rows, axis=-2)
    strip = jnp.concatenate([mixed[:, b] for b in range(3)], axis=-1)
    unit = 2 * ins
    bands = [
        jnp.pad(strip, ((0, 0), (0, 0), (0, 0), (unit * x, unit * (BLOCK - 1 - x)))) for x in range(BLOCK)
    ]
    return jnp.concatenate(bands, axis=-2)


def mixer_weights(mixers):
    layers, outs, ins = mixers.shape
    times = 2 * BLOCK
    eye = jnp.eye(times, dtype=mixers.dtype)
    spread = mixers[:, None, :, None, :] * eye[None, :, None, :, None]
    return spread.reshape(layers, times * outs, times * ins)


def couplings_body(layers, rows, width, lanes, total_rows, total_cols, unit,
                   place_ref, cells_ref, weight_ref, mixer_ref, bias_ref, out_ref, halves, shifted):
    halo_rows = rows + 2 * HALO
    row_start = place_ref[0] - HALO
    col_start = place_ref[1]
    lane = lax.broadcasted_iota(jnp.int32, (1, lanes), 1)
    column = jnp.where(lane >= lanes - HALO, lane - lanes, lane) + col_start
    column_ok = jnp.where((column >= 0) & (column < total_cols), 1.0, 0.0)
    for half in range(2):
        halves[half, 0:halo_rows * unit, :] = cells_ref[half]
        halves[half, halo_rows * unit:, :] = jnp.zeros(
            (halves.shape[1] - halo_rows * unit, lanes), halves.dtype)
        for side in range(2):
            shifted[2 * side, halo_rows * unit:, :] = jnp.zeros(
                (halves.shape[1] - halo_rows * unit, lanes), halves.dtype)
    for layer in range(layers):
        source, target = layer % 2, 1 - layer % 2

        def spread(index, _, source=source):
            at = pl.ds(pl.multiple_of(index * unit, unit), unit)
            line = halves[source, at, :].astype(jnp.float32)
            shifted[0, at, :] = pltpu.roll(line, 1, 1).astype(jnp.bfloat16)
            shifted[1, at, :] = halves[source, at, :]
            shifted[2, at, :] = pltpu.roll(line, lanes - 1, 1).astype(jnp.bfloat16)
            return 0

        lax.fori_loop(0, halves.shape[1] // unit, spread, 0)
        left = halo_rows - 2 * layer - 2
        steps = -(-left // BLOCK)

        def block(index, _, layer=layer, target=target):
            start = layer + index * BLOCK
            inside = pl.ds(pl.multiple_of(start * unit, unit), (BLOCK + 2) * unit)
            raw = jnp.dot(weight_ref[layer, 0], shifted[0, inside, :], preferred_element_type=jnp.float32)
            raw += jnp.dot(weight_ref[layer, 1], shifted[1, inside, :], preferred_element_type=jnp.float32)
            raw += jnp.dot(weight_ref[layer, 2], shifted[2, inside, :], preferred_element_type=jnp.float32)
            hidden = jnp.maximum(raw + bias_ref[layer], 0.0)
            step = lax.broadcasted_iota(jnp.int32, (BLOCK * unit, 1), 0) // unit
            row = step + (start + 1 + row_start)
            row_ok = jnp.where((row >= 0) & (row < total_rows), 1.0, 0.0)
            hidden = (hidden * row_ok * column_ok).astype(jnp.bfloat16)
            update = jnp.dot(mixer_ref[layer], hidden, preferred_element_type=jnp.float32)
            at = pl.ds(pl.multiple_of((start + 1) * unit, unit), BLOCK * unit)
            halves[target, at, :] = (halves[target, at, :].astype(jnp.float32) + update).astype(jnp.bfloat16)
            return 0

        lax.fori_loop(0, steps, block, 0)
    for half in range(2):
        out_ref[half] = halves[half, HALO * unit:(HALO + rows) * unit, 0:width]


def couple(merged, kernels, biases, mixers, total_rows, total_cols):
    channels, positions, rows, width = merged.shape
    half = channels // 2
    layers = kernels.shape[0]
    unit = half * positions
    lanes = -(-(width + 2 * HALO) // 128) * 128
    cells = jnp.transpose(merged.reshape(2, half, positions, rows, width), (0, 3, 2, 1, 4))
    cells = cells.reshape(2, rows, unit, width)
    count = lax.axis_size("coil")
    up = [(i, i + 1) for i in range(count - 1)]
    down = [(i + 1, i) for i in range(count - 1)]
    before = lax.ppermute(cells[..., width - HALO:], "coil", up)
    after = lax.ppermute(cells[..., :HALO], "coil", down)
    gap = jnp.zeros(cells.shape[:-1] + (lanes - width - 2 * HALO,), cells.dtype)
    cells = jnp.concatenate([cells, after, gap, before], axis=-1)
    count = lax.axis_size("space")
    up = [(i, i + 1) for i in range(count - 1)]
    down = [(i + 1, i) for i in range(count - 1)]
    above = lax.ppermute(cells[:, rows - HALO:], "space", up)
    below = lax.ppermute(cells[:, :HALO], "space", down)
    cells = jnp.concatenate([above, cells, below], axis=1)
    halo_rows = rows + 2 * HALO
    held = halo_rows + 8
    cells = cells.reshape(2, halo_rows * unit, lanes)
    place = jnp.stack([lax.axis_index("space") * rows, lax.axis_index("coil") * width]).astype(jnp.int32)
    bias = jnp.tile(biases, (1, positions * BLOCK))[:, :, None]
    vmem = pl.BlockSpec(memory_space=pltpu.VMEM)
    out = pl.pallas_call(
        functools.partial(couplings_body, layers, rows, width, lanes, total_rows, total_cols, unit),
        out_shape=jax.ShapeDtypeStruct((2, rows * unit, width), jnp.bfloat16),
        in_specs=[pl.BlockSpec(memory_space=pltpu.SMEM)] + [vmem] * 4,
        out_specs=vmem,
        scratch_shapes=[
            pltpu.VMEM((2, held * unit, lanes), jnp.bfloat16),
            pltpu.VMEM((3, held * unit, lanes), jnp.bfloat16),
        ],
        compiler_params=pltpu.CompilerParams(vmem_limit_bytes=56 * 1024 * 1024),
    )(place, cells, coupling_weights(kernels), mixer_weights(mixers), bias)
    out = out.reshape(2, rows, positions, half, width)
    return jnp.transpose(out, (0, 3, 2, 1, 4)).reshape(channels, positions, rows, width)


def per_device(state, sens, kdata, mask, inject, kernels, biases, mixers):
    npar = sens.shape[4]
    npe = kdata.shape[4]
    estimate = lax.all_gather(state[0:2], "coil", axis=3, tiled=True).astype(jnp.float32)
    coil_real = sens[0] * estimate[0][None] - sens[1] * estimate[1][None]
    coil_imag = sens[0] * estimate[1][None] + sens[1] * estimate[0][None]
    coil_images = jnp.stack([coil_real, coil_imag])
    par_table = dft_table(npar)
    pe_table = dft_table(npe)
    columns_done = transform(coil_images, par_table, npar, -1.0, "rcpqn,nk->rcpqk")
    spectra = lax.all_to_all(
        columns_done.astype(jnp.bfloat16), "space", split_axis=4, concat_axis=3, tiled=True
    ).astype(columns_done.dtype)
    full = transform(spectra, pe_table, npe, -1.0, "rcpnq,nk->rcpqk")
    sampled = mask.astype(jnp.float32)
    residual = sampled * (full - kdata)
    lines = transform(residual, pe_table, npe, 1.0, "rcpqk,kn->rcpqn")
    returned = lax.all_to_all(
        lines.astype(jnp.bfloat16), "space", split_axis=4, concat_axis=3, tiled=True
    ).astype(lines.dtype)
    images = transform(returned, par_table, npar, 1.0, "rcpkn,kq->rcpnq")
    part_real = jnp.sum(sens[0] * images[0] + sens[1] * images[1], axis=0)
    part_imag = jnp.sum(sens[0] * images[1] - sens[1] * images[0], axis=0)
    gradient = lax.psum_scatter(
        jnp.stack([part_real, part_imag]).astype(jnp.bfloat16),
        "coil",
        scatter_dimension=3,
        tiled=True,
    ).astype(jnp.float32)
    added = jnp.einsum("cg,gpqr->cpqr", inject, gradient, precision=lax.Precision.HIGHEST)
    merged = (state.astype(jnp.float32) + added).astype(jnp.bfloat16)
    new_state = couple(merged, kernels, biases, mixers, npe, npar)
    return (new_state, gradient)


def solution(mesh):
    return jax.shard_map(
        per_device,
        mesh=mesh,
        in_specs=(
            P(None, None, "space", "coil"),
            P(None, "coil", None, "space", None),
            P(None, "coil", None, "space", None),
            P("space", None),
            P(),
            P(),
            P(),
            P(),
        ),
        out_specs=(P(None, None, "space", "coil"), P(None, None, "space", "coil")),
        check_vma=False,
    )
```

```python
import functools
import math

import jax
import jax.numpy as jnp
from jax import lax
from jax.experimental import pallas as pl
from jax.experimental.pallas import tpu as pltpu
from jax.sharding import PartitionSpec as P


def dft_table(length):
    inner = 32
    column = lax.iota(jnp.int32, length)[None, :]
    fine = lax.iota(jnp.int32, inner)[:, None] * column % length
    coarse = (lax.iota(jnp.int32, length // inner)[:, None] * inner) * column % length
    unit = 2.0 * math.pi / length
    fine = fine.astype(jnp.float32) * unit
    coarse = coarse.astype(jnp.float32) * unit
    scale = 1.0 / math.sqrt(length)
    fine_cos, fine_sin, coarse_cos, coarse_sin = lax.optimization_barrier(
        (jnp.cos(fine), jnp.sin(fine), jnp.cos(coarse) * scale, jnp.sin(coarse) * scale)
    )
    fine_cos, fine_sin = fine_cos[None], fine_sin[None]
    coarse_cos, coarse_sin = coarse_cos[:, None], coarse_sin[:, None]
    table = jnp.stack([coarse_cos * fine_cos - coarse_sin * fine_sin, coarse_sin * fine_cos + coarse_cos * fine_sin])
    return table.astype(jnp.bfloat16).reshape(2, length, length)


def gradient_body(spaces, coils, estimate_ref, sens_ref, kdata_ref, mask_ref, par_ref, pe_ref, out_ref,
                  seen, whole, send_out, got_out, send_back, got_back, total, part, parts,
                  seen_sent, seen_got, out_sent, out_got, back_sent, back_got, part_sent, part_got):
    space = lax.axis_index("space")
    coil = lax.axis_index("coil")
    f32, bf16 = jnp.float32, jnp.bfloat16
    width = estimate_ref.shape[2]
    count, positions, rows, npar = sens_ref.shape[1:]
    held, npe = kdata_ref.shape[3:]
    sites = positions * rows
    lines = positions * held

    barrier = pltpu.get_barrier_semaphore()

    @pl.loop(1, spaces)
    def _(offset):
        pl.semaphore_signal(barrier, inc=1, device_id={"space": lax.rem(space + offset, spaces)},
                            device_id_type=pl.DeviceIdType.MESH)

    for offset in range(1, coils):
        pl.semaphore_signal(barrier, inc=1, device_id={"coil": lax.rem(coil + offset, coils)},
                            device_id_type=pl.DeviceIdType.MESH)
    pl.semaphore_wait(barrier, spaces + coils - 2)

    def to_coil(source, target, offset, sent, got):
        return pltpu.make_async_remote_copy(
            src_ref=source, dst_ref=target, send_sem=sent.at[offset], recv_sem=got.at[offset],
            device_id={"coil": lax.rem(coil + offset, coils)}, device_id_type=pl.DeviceIdType.MESH)

    def to_space(buffer, target, c, offset, sent, got):
        other = lax.rem(space + offset, spaces)
        return pltpu.make_async_remote_copy(
            src_ref=buffer.at[c, other], dst_ref=target.at[c, space], send_sem=sent.at[c], recv_sem=got.at[c],
            device_id={"space": other}, device_id_type=pl.DeviceIdType.MESH)

    def all_of(buffer, c, sem):
        span = buffer.at[c, pl.ds(0, spaces - 1)]
        pltpu.make_async_copy(span, span, sem.at[c]).wait()

    for offset in range(1, coils):
        to_coil(estimate_ref, seen.at[coil], offset, seen_sent, seen_got).start()
    seen[coil] = estimate_ref[...]
    for offset in range(1, coils):
        to_coil(estimate_ref, seen.at[coil], offset, seen_sent, seen_got).wait()
    for part_of in range(2):
        whole[part_of] = jnp.concatenate([seen[j, part_of].astype(f32) for j in range(coils)], axis=-1)

    @pl.loop(0, count)
    def _(c):
        profile_real = sens_ref[0, c].reshape(sites, npar)
        profile_imag = sens_ref[1, c].reshape(sites, npar)
        real = profile_real * whole[0] - profile_imag * whole[1]
        imag = profile_real * whole[1] + profile_imag * whole[0]
        plain = jnp.concatenate([real, imag], axis=0).astype(bf16)
        turned = jnp.concatenate([imag, -real], axis=0).astype(bf16)
        along = (((1,), (1,)), ((), ()))
        spectrum = lax.dot_general(par_ref[0], plain, along, preferred_element_type=f32)
        spectrum += lax.dot_general(par_ref[1], turned, along, preferred_element_type=f32)
        send_out[c] = spectrum.reshape(spaces, held, 2 * sites).astype(bf16)

        @pl.loop(1, spaces)
        def _(offset):
            to_space(send_out, got_out, c, offset, out_sent, out_got).start()

        got_out[c, space] = send_out[c, space]

    @pl.loop(0, count)
    def _(c):
        all_of(got_out, c, out_got)
        blocks = [got_out[c, s].astype(f32) for s in range(spaces)]
        grid = [
            jnp.concatenate([block[:, k * rows:(k + 1) * rows] for block in blocks], axis=-1)
            for k in range(2 * positions)
        ]
        real = jnp.concatenate(grid[:positions], axis=0)
        imag = jnp.concatenate(grid[positions:], axis=0)
        plain = jnp.concatenate([real, imag], axis=0).astype(bf16)
        turned = jnp.concatenate([imag, -real], axis=0).astype(bf16)
        full = jnp.dot(plain, pe_ref[0], preferred_element_type=f32)
        full += jnp.dot(turned, pe_ref[1], preferred_element_type=f32)
        sampled = jnp.concatenate([mask_ref[...].astype(f32)] * positions, axis=0)
        real = sampled * (full[:lines] - kdata_ref[0, c].reshape(lines, npe))
        imag = sampled * (full[lines:] - kdata_ref[1, c].reshape(lines, npe))
        plain = jnp.concatenate([real, imag], axis=0).astype(bf16)
        turned = jnp.concatenate([-imag, real], axis=0).astype(bf16)
        back = jnp.dot(plain, pe_ref[0], preferred_element_type=f32)
        back += jnp.dot(turned, pe_ref[1], preferred_element_type=f32)
        for s in range(spaces):
            send_back[c, s] = jnp.concatenate(
                [back[k * held:(k + 1) * held, s * rows:(s + 1) * rows] for k in range(2 * positions)], axis=-1
            ).astype(bf16)

        @pl.loop(1, spaces)
        def _(offset):
            to_space(send_back, got_back, c, offset, back_sent, back_got).start()

        got_back[c, space] = send_back[c, space]

    total[...] = jnp.zeros_like(total)

    @pl.loop(0, count)
    def _(c):
        all_of(got_back, c, back_got)
        plain = got_back[c].astype(f32).reshape(npar, 2 * sites)
        turned = jnp.concatenate([-plain[:, sites:], plain[:, :sites]], axis=-1).astype(bf16)
        along = (((0,), (0,)), ((), ()))
        image = lax.dot_general(plain.astype(bf16), par_ref[0], along, preferred_element_type=f32)
        image += lax.dot_general(turned, par_ref[1], along, preferred_element_type=f32)
        real, imag = image[:sites], image[sites:]
        profile_real = sens_ref[0, c].reshape(sites, npar)
        profile_imag = sens_ref[1, c].reshape(sites, npar)
        total[0] += profile_real * real + profile_imag * imag
        total[1] += profile_real * imag - profile_imag * real

    for j in range(coils):
        for part_of in range(2):
            part[j, part_of] = total[part_of, :, j * width:(j + 1) * width].astype(bf16)
    for offset in range(1, coils):
        to_coil(part.at[lax.rem(coil + offset, coils)], parts.at[coil], offset, part_sent, part_got).start()
    parts[coil] = part[coil]
    for offset in range(1, coils):
        to_coil(part.at[lax.rem(coil + offset, coils)], parts.at[coil], offset, part_sent, part_got).wait()
    result = parts[0].astype(f32)
    for j in range(1, coils):
        result += parts[j].astype(f32)
    out_ref[...] = result

    @pl.loop(0, count)
    def _(c):
        all_of(send_out, c, out_sent)
        all_of(send_back, c, back_sent)


def find_gradient(state, sens, kdata, mask):
    spaces, coils = lax.axis_size("space"), lax.axis_size("coil")
    _, positions, rows, width = state.shape
    count, npar = sens.shape[1], sens.shape[4]
    held, npe = kdata.shape[3:]
    sites = positions * rows
    bf16, f32 = jnp.bfloat16, jnp.float32
    vmem = pl.BlockSpec(memory_space=pltpu.VMEM)
    dma = pltpu.SemaphoreType.DMA
    message = pltpu.VMEM((count, spaces, held, 2 * sites), bf16)
    result = pl.pallas_call(
        functools.partial(gradient_body, spaces, coils),
        out_shape=jax.ShapeDtypeStruct((2, sites, width), f32),
        in_specs=[vmem] * 6,
        out_specs=vmem,
        scratch_shapes=[
            pltpu.VMEM((coils, 2, sites, width), bf16),
            pltpu.VMEM((2, sites, npar), f32),
            message, message, message, message,
            pltpu.VMEM((2, sites, npar), f32),
            pltpu.VMEM((coils, 2, sites, width), bf16),
            pltpu.VMEM((coils, 2, sites, width), bf16),
            dma((coils,)), dma((coils,)), dma((count,)), dma((count,)),
            dma((count,)), dma((count,)), dma((coils,)), dma((coils,)),
        ],
        compiler_params=pltpu.CompilerParams(
            collective_id=0, has_side_effects=True, vmem_limit_bytes=60 * 1024 * 1024),
    )(state[0:2].reshape(2, sites, width), sens, kdata, mask, dft_table(npar), dft_table(npe))
    return result.reshape(2, positions, rows, width)


HALO = 4
BLOCK = 6


def coupling_weights(kernels):
    layers, _, outs, ins = kernels.shape
    taps = kernels.reshape(layers, 3, 3, 3, outs, ins)
    rows = []
    for out_pos in range(2):
        rows.append(jnp.concatenate([taps[:, in_pos - out_pos + 1] for in_pos in range(2)], axis=-1))
    mixed = jnp.concatenate(rows, axis=-2)
    strip = jnp.concatenate([mixed[:, b] for b in range(3)], axis=-1)
    unit = 2 * ins
    bands = [
        jnp.pad(strip, ((0, 0), (0, 0), (0, 0), (unit * x, unit * (BLOCK - 1 - x)))) for x in range(BLOCK)
    ]
    return jnp.concatenate(bands, axis=-2)


def mixer_weights(mixers):
    layers, outs, ins = mixers.shape
    times = 2 * BLOCK
    eye = jnp.eye(times, dtype=mixers.dtype)
    spread = mixers[:, None, :, None, :] * eye[None, :, None, :, None]
    return spread.reshape(layers, times * outs, times * ins)


def couplings_body(layers, rows, width, lanes, total_rows, total_cols, unit,
                   place_ref, cells_ref, weight_ref, mixer_ref, bias_ref, out_ref, halves, shifted):
    halo_rows = rows + 2 * HALO
    row_start = place_ref[0] - HALO
    col_start = place_ref[1]
    lane = lax.broadcasted_iota(jnp.int32, (1, lanes), 1)
    column = jnp.where(lane >= lanes - HALO, lane - lanes, lane) + col_start
    column_ok = jnp.where((column >= 0) & (column < total_cols), 1.0, 0.0)
    for half in range(2):
        halves[half, 0:halo_rows * unit, :] = cells_ref[half]
        halves[half, halo_rows * unit:, :] = jnp.zeros(
            (halves.shape[1] - halo_rows * unit, lanes), halves.dtype)
        for side in range(2):
            shifted[2 * side, halo_rows * unit:, :] = jnp.zeros(
                (halves.shape[1] - halo_rows * unit, lanes), halves.dtype)
    for layer in range(layers):
        source, target = layer % 2, 1 - layer % 2

        def spread(index, _, source=source):
            at = pl.ds(pl.multiple_of(index * unit, unit), unit)
            line = halves[source, at, :].astype(jnp.float32)
            shifted[0, at, :] = pltpu.roll(line, 1, 1).astype(jnp.bfloat16)
            shifted[1, at, :] = halves[source, at, :]
            shifted[2, at, :] = pltpu.roll(line, lanes - 1, 1).astype(jnp.bfloat16)
            return 0

        lax.fori_loop(0, halves.shape[1] // unit, spread, 0)
        left = halo_rows - 2 * layer - 2
        steps = -(-left // BLOCK)

        def block(index, _, layer=layer, target=target):
            start = layer + index * BLOCK
            inside = pl.ds(pl.multiple_of(start * unit, unit), (BLOCK + 2) * unit)
            raw = jnp.dot(weight_ref[layer, 0], shifted[0, inside, :], preferred_element_type=jnp.float32)
            raw += jnp.dot(weight_ref[layer, 1], shifted[1, inside, :], preferred_element_type=jnp.float32)
            raw += jnp.dot(weight_ref[layer, 2], shifted[2, inside, :], preferred_element_type=jnp.float32)
            hidden = jnp.maximum(raw + bias_ref[layer], 0.0)
            step = lax.broadcasted_iota(jnp.int32, (BLOCK * unit, 1), 0) // unit
            row = step + (start + 1 + row_start)
            row_ok = jnp.where((row >= 0) & (row < total_rows), 1.0, 0.0)
            hidden = (hidden * row_ok * column_ok).astype(jnp.bfloat16)
            update = jnp.dot(mixer_ref[layer], hidden, preferred_element_type=jnp.float32)
            at = pl.ds(pl.multiple_of((start + 1) * unit, unit), BLOCK * unit)
            halves[target, at, :] = (halves[target, at, :].astype(jnp.float32) + update).astype(jnp.bfloat16)
            return 0

        lax.fori_loop(0, steps, block, 0)
    for half in range(2):
        out_ref[half] = halves[half, HALO * unit:(HALO + rows) * unit, 0:width]


def couple(merged, kernels, biases, mixers, total_rows, total_cols):
    channels, positions, rows, width = merged.shape
    half = channels // 2
    layers = kernels.shape[0]
    unit = half * positions
    lanes = -(-(width + 2 * HALO) // 128) * 128
    cells = jnp.transpose(merged.reshape(2, half, positions, rows, width), (0, 3, 2, 1, 4))
    cells = cells.reshape(2, rows, unit, width)
    count = lax.axis_size("coil")
    up = [(i, i + 1) for i in range(count - 1)]
    down = [(i + 1, i) for i in range(count - 1)]
    before = lax.ppermute(cells[..., width - HALO:], "coil", up)
    after = lax.ppermute(cells[..., :HALO], "coil", down)
    gap = jnp.zeros(cells.shape[:-1] + (lanes - width - 2 * HALO,), cells.dtype)
    cells = jnp.concatenate([cells, after, gap, before], axis=-1)
    count = lax.axis_size("space")
    up = [(i, i + 1) for i in range(count - 1)]
    down = [(i + 1, i) for i in range(count - 1)]
    above = lax.ppermute(cells[:, rows - HALO:], "space", up)
    below = lax.ppermute(cells[:, :HALO], "space", down)
    cells = jnp.concatenate([above, cells, below], axis=1)
    halo_rows = rows + 2 * HALO
    held = halo_rows + 8
    cells = cells.reshape(2, halo_rows * unit, lanes)
    place = jnp.stack([lax.axis_index("space") * rows, lax.axis_index("coil") * width]).astype(jnp.int32)
    bias = jnp.tile(biases, (1, positions * BLOCK))[:, :, None]
    vmem = pl.BlockSpec(memory_space=pltpu.VMEM)
    out = pl.pallas_call(
        functools.partial(couplings_body, layers, rows, width, lanes, total_rows, total_cols, unit),
        out_shape=jax.ShapeDtypeStruct((2, rows * unit, width), jnp.bfloat16),
        in_specs=[pl.BlockSpec(memory_space=pltpu.SMEM)] + [vmem] * 4,
        out_specs=vmem,
        scratch_shapes=[
            pltpu.VMEM((2, held * unit, lanes), jnp.bfloat16),
            pltpu.VMEM((3, held * unit, lanes), jnp.bfloat16),
        ],
        compiler_params=pltpu.CompilerParams(vmem_limit_bytes=56 * 1024 * 1024),
    )(place, cells, coupling_weights(kernels), mixer_weights(mixers), bias)
    out = out.reshape(2, rows, positions, half, width)
    return jnp.transpose(out, (0, 3, 2, 1, 4)).reshape(channels, positions, rows, width)


def per_device(state, sens, kdata, mask, inject, kernels, biases, mixers):
    npar = sens.shape[4]
    npe = kdata.shape[4]
    gradient = find_gradient(state, sens, kdata, mask)
    added = jnp.einsum("cg,gpqr->cpqr", inject, gradient, precision=lax.Precision.HIGHEST)
    merged = (state.astype(jnp.float32) + added).astype(jnp.bfloat16)
    new_state = couple(merged, kernels, biases, mixers, npe, npar)
    return (new_state, gradient)


def solution(mesh):
    return jax.shard_map(
        per_device,
        mesh=mesh,
        in_specs=(
            P(None, None, "space", "coil"),
            P(None, "coil", None, "space", None),
            P(None, "coil", None, "space", None),
            P("space", None),
            P(),
            P(),
            P(),
            P(),
        ),
        out_specs=(P(None, None, "space", "coil"), P(None, None, "space", "coil")),
        check_vma=False,
    )
```

```python
import functools
import math

import jax
import jax.numpy as jnp
from jax import lax
from jax.experimental import pallas as pl
from jax.experimental.pallas import tpu as pltpu
from jax.sharding import PartitionSpec as P


def dft_table(length):
    inner = 32
    column = lax.iota(jnp.int32, length)[None, :]
    fine = lax.iota(jnp.int32, inner)[:, None] * column % length
    coarse = (lax.iota(jnp.int32, length // inner)[:, None] * inner) * column % length
    unit = 2.0 * math.pi / length
    fine = fine.astype(jnp.float32) * unit
    coarse = coarse.astype(jnp.float32) * unit
    scale = 1.0 / math.sqrt(length)
    fine_cos, fine_sin, coarse_cos, coarse_sin = lax.optimization_barrier(
        (jnp.cos(fine), jnp.sin(fine), jnp.cos(coarse) * scale, jnp.sin(coarse) * scale)
    )
    fine_cos, fine_sin = fine_cos[None], fine_sin[None]
    coarse_cos, coarse_sin = coarse_cos[:, None], coarse_sin[:, None]
    table = jnp.stack([coarse_cos * fine_cos - coarse_sin * fine_sin, coarse_sin * fine_cos + coarse_cos * fine_sin])
    return table.astype(jnp.bfloat16).reshape(2, length, length)


def gradient_body(spaces, coils, estimate_ref, sens_ref, kdata_ref, mask_ref, par_ref, pe_ref, state_ref, out_ref, cells_ref,
                  seen, whole, send_out, got_out, send_back, got_back, total, part, parts,
                  seen_sent, seen_got, out_sent, out_got, back_sent, back_got, part_sent, part_got):
    space = lax.axis_index("space")
    coil = lax.axis_index("coil")
    f32, bf16 = jnp.float32, jnp.bfloat16
    width = estimate_ref.shape[2]
    count, positions, rows, npar = sens_ref.shape[1:]
    held, npe = kdata_ref.shape[3:]
    sites = positions * rows
    lines = positions * held

    barrier = pltpu.get_barrier_semaphore()

    @pl.loop(1, spaces)
    def _(offset):
        pl.semaphore_signal(barrier, inc=1, device_id={"space": lax.rem(space + offset, spaces)},
                            device_id_type=pl.DeviceIdType.MESH)

    for offset in range(1, coils):
        pl.semaphore_signal(barrier, inc=1, device_id={"coil": lax.rem(coil + offset, coils)},
                            device_id_type=pl.DeviceIdType.MESH)
    pl.semaphore_wait(barrier, spaces + coils - 2)

    def to_coil(source, target, offset, sent, got):
        return pltpu.make_async_remote_copy(
            src_ref=source, dst_ref=target, send_sem=sent.at[offset], recv_sem=got.at[offset],
            device_id={"coil": lax.rem(coil + offset, coils)}, device_id_type=pl.DeviceIdType.MESH)

    def to_space(buffer, target, c, offset, sent, got):
        other = lax.rem(space + offset, spaces)
        return pltpu.make_async_remote_copy(
            src_ref=buffer.at[c, other], dst_ref=target.at[c, space], send_sem=sent.at[c], recv_sem=got.at[c],
            device_id={"space": other}, device_id_type=pl.DeviceIdType.MESH)

    def all_of(buffer, c, sem):
        span = buffer.at[c, pl.ds(0, spaces - 1)]
        pltpu.make_async_copy(span, span, sem.at[c]).wait()

    for offset in range(1, coils):
        to_coil(estimate_ref, seen.at[coil], offset, seen_sent, seen_got).start()
    seen[coil] = estimate_ref[...]
    for offset in range(1, coils):
        to_coil(estimate_ref, seen.at[coil], offset, seen_sent, seen_got).wait()
    for part_of in range(2):
        whole[part_of] = jnp.concatenate([seen[j, part_of].astype(f32) for j in range(coils)], axis=-1)

    @pl.loop(0, count)
    def _(c):
        profile_real = sens_ref[0, c].reshape(sites, npar)
        profile_imag = sens_ref[1, c].reshape(sites, npar)
        real = profile_real * whole[0] - profile_imag * whole[1]
        imag = profile_real * whole[1] + profile_imag * whole[0]
        plain = jnp.concatenate([real, imag], axis=0).astype(bf16)
        turned = jnp.concatenate([imag, -real], axis=0).astype(bf16)
        along = (((1,), (1,)), ((), ()))
        spectrum = lax.dot_general(par_ref[0], plain, along, preferred_element_type=f32)
        spectrum += lax.dot_general(par_ref[1], turned, along, preferred_element_type=f32)
        send_out[c] = spectrum.reshape(spaces, held, 2 * sites).astype(bf16)

        @pl.loop(1, spaces)
        def _(offset):
            to_space(send_out, got_out, c, offset, out_sent, out_got).start()

        got_out[c, space] = send_out[c, space]

    half = state_ref.shape[0] // 2
    group = 16

    @pl.loop(0, rows // group)
    def _(g):
        at = pl.ds(pl.multiple_of(g * group, group), group)
        for side in range(2):
            for position in range(positions):
                cells = state_ref[side * half:(side + 1) * half, position, at, :].astype(f32)
                cells_ref[side, at, position * half:(position + 1) * half, :] = jnp.swapaxes(cells, 0, 1).astype(bf16)

    @pl.loop(0, count)
    def _(c):
        all_of(got_out, c, out_got)
        blocks = [got_out[c, s].astype(f32) for s in range(spaces)]
        grid = [
            jnp.concatenate([block[:, k * rows:(k + 1) * rows] for block in blocks], axis=-1)
            for k in range(2 * positions)
        ]
        real = jnp.concatenate(grid[:positions], axis=0)
        imag = jnp.concatenate(grid[positions:], axis=0)
        plain = jnp.concatenate([real, imag], axis=0).astype(bf16)
        turned = jnp.concatenate([imag, -real], axis=0).astype(bf16)
        full = jnp.dot(plain, pe_ref[0], preferred_element_type=f32)
        full += jnp.dot(turned, pe_ref[1], preferred_element_type=f32)
        sampled = jnp.concatenate([mask_ref[...].astype(f32)] * positions, axis=0)
        real = sampled * (full[:lines] - kdata_ref[0, c].reshape(lines, npe))
        imag = sampled * (full[lines:] - kdata_ref[1, c].reshape(lines, npe))
        plain = jnp.concatenate([real, imag], axis=0).astype(bf16)
        turned = jnp.concatenate([-imag, real], axis=0).astype(bf16)
        back = jnp.dot(plain, pe_ref[0], preferred_element_type=f32)
        back += jnp.dot(turned, pe_ref[1], preferred_element_type=f32)
        for s in range(spaces):
            send_back[c, s] = jnp.concatenate(
                [back[k * held:(k + 1) * held, s * rows:(s + 1) * rows] for k in range(2 * positions)], axis=-1
            ).astype(bf16)

        @pl.loop(1, spaces)
        def _(offset):
            to_space(send_back, got_back, c, offset, back_sent, back_got).start()

        got_back[c, space] = send_back[c, space]

    total[...] = jnp.zeros_like(total)

    @pl.loop(0, count)
    def _(c):
        all_of(got_back, c, back_got)
        plain = got_back[c].astype(f32).reshape(npar, 2 * sites)
        turned = jnp.concatenate([-plain[:, sites:], plain[:, :sites]], axis=-1).astype(bf16)
        along = (((0,), (0,)), ((), ()))
        image = lax.dot_general(plain.astype(bf16), par_ref[0], along, preferred_element_type=f32)
        image += lax.dot_general(turned, par_ref[1], along, preferred_element_type=f32)
        real, imag = image[:sites], image[sites:]
        profile_real = sens_ref[0, c].reshape(sites, npar)
        profile_imag = sens_ref[1, c].reshape(sites, npar)
        total[0] += profile_real * real + profile_imag * imag
        total[1] += profile_real * imag - profile_imag * real

    for j in range(coils):
        for part_of in range(2):
            part[j, part_of] = total[part_of, :, j * width:(j + 1) * width].astype(bf16)
    for offset in range(1, coils):
        to_coil(part.at[lax.rem(coil + offset, coils)], parts.at[coil], offset, part_sent, part_got).start()
    parts[coil] = part[coil]
    for offset in range(1, coils):
        to_coil(part.at[lax.rem(coil + offset, coils)], parts.at[coil], offset, part_sent, part_got).wait()
    result = parts[0].astype(f32)
    for j in range(1, coils):
        result += parts[j].astype(f32)
    out_ref[...] = result

    @pl.loop(0, count)
    def _(c):
        all_of(send_out, c, out_sent)
        all_of(send_back, c, back_sent)


def find_gradient(state, sens, kdata, mask):
    spaces, coils = lax.axis_size("space"), lax.axis_size("coil")
    _, positions, rows, width = state.shape
    count, npar = sens.shape[1], sens.shape[4]
    held, npe = kdata.shape[3:]
    sites = positions * rows
    bf16, f32 = jnp.bfloat16, jnp.float32
    vmem = pl.BlockSpec(memory_space=pltpu.VMEM)
    dma = pltpu.SemaphoreType.DMA
    message = pltpu.VMEM((count, spaces, held, 2 * sites), bf16)
    channels = state.shape[0]
    result, cells = pl.pallas_call(
        functools.partial(gradient_body, spaces, coils),
        out_shape=(
            jax.ShapeDtypeStruct((2, sites, width), f32),
            jax.ShapeDtypeStruct((2, rows, positions * channels // 2, width), bf16),
        ),
        in_specs=[vmem] * 7,
        out_specs=(vmem, vmem),
        scratch_shapes=[
            pltpu.VMEM((coils, 2, sites, width), bf16),
            pltpu.VMEM((2, sites, npar), f32),
            message, message, message, message,
            pltpu.VMEM((2, sites, npar), f32),
            pltpu.VMEM((coils, 2, sites, width), bf16),
            pltpu.VMEM((coils, 2, sites, width), bf16),
            dma((coils,)), dma((coils,)), dma((count,)), dma((count,)),
            dma((count,)), dma((count,)), dma((coils,)), dma((coils,)),
        ],
        compiler_params=pltpu.CompilerParams(
            collective_id=0, has_side_effects=True, vmem_limit_bytes=60 * 1024 * 1024),
    )(state[0:2].reshape(2, sites, width), sens, kdata, mask, dft_table(npar), dft_table(npe), state)
    return result.reshape(2, positions, rows, width), cells


HALO = 4
BLOCK = 6


def coupling_weights(kernels):
    layers, _, outs, ins = kernels.shape
    taps = kernels.reshape(layers, 3, 3, 3, outs, ins)
    rows = []
    for out_pos in range(2):
        rows.append(jnp.concatenate([taps[:, in_pos - out_pos + 1] for in_pos in range(2)], axis=-1))
    mixed = jnp.concatenate(rows, axis=-2)
    strip = jnp.concatenate([mixed[:, b, c] for b in range(3) for c in range(3)], axis=-1)
    unit = 6 * ins
    bands = [
        jnp.pad(strip, ((0, 0), (0, 0), (unit * x, unit * (BLOCK - 1 - x)))) for x in range(BLOCK)
    ]
    return jnp.concatenate(bands, axis=-2)


def mixer_weights(mixers):
    ins = mixers.shape[2]
    times = 2 * BLOCK
    bands = [jnp.pad(mixers, ((0, 0), (0, 0), (ins * x, ins * (times - 1 - x)))) for x in range(times)]
    return jnp.concatenate(bands, axis=-2)


def couplings_body(layers, rows, width, lanes, total_rows, total_cols, unit, spaces, coils,
                   cells_ref, gradient_ref, inject_ref, weight_ref, mixer_ref, bias_ref, out_ref,
                   halves, shifted, strips, borders, col_sent, col_got, row_sent, row_got):
    f32, bf16 = jnp.float32, jnp.bfloat16
    mesh_id = pl.DeviceIdType.MESH
    space = lax.axis_index("space")
    coil = lax.axis_index("coil")
    positions = gradient_ref.shape[1]
    halo_rows = rows + 2 * HALO
    row_start = space * rows - HALO
    col_start = coil * width

    barrier = pltpu.get_barrier_semaphore()
    for step in (1, -1):
        pl.semaphore_signal(barrier, inc=1, device_id={"coil": lax.rem(coil + step + coils, coils)}, device_id_type=mesh_id)
        pl.semaphore_signal(barrier, inc=1, device_id={"space": lax.rem(space + step + spaces, spaces)}, device_id_type=mesh_id)
    pl.semaphore_wait(barrier, 4)

    for half in range(2):
        spare = (halves.shape[1] - halo_rows * unit, lanes)
        halves[half, halo_rows * unit:, :] = jnp.zeros(spare, bf16)

        @pl.when(space == 0)
        def _(half=half):
            halves[half, 0:HALO * unit, :] = jnp.zeros((HALO * unit, lanes), bf16)

        @pl.when(space == spaces - 1)
        def _(half=half):
            halves[half, (HALO + rows) * unit:halo_rows * unit, :] = jnp.zeros((HALO * unit, lanes), bf16)

    @pl.loop(0, rows)
    def _(row):
        lines = [
            jnp.concatenate(
                [
                    jnp.broadcast_to(gradient_ref[g, p, pl.ds(row, 1), :], (unit // positions, width))
                    for p in range(positions)
                ],
                axis=0,
            )
            for g in range(2)
        ]
        from_row = pl.ds(pl.multiple_of(row * unit, unit), unit)
        into = pl.ds(pl.multiple_of((row + HALO) * unit, unit), unit)
        for half in range(2):
            added = inject_ref[half, 0] * lines[0] + inject_ref[half, 1] * lines[1]
            merged = cells_ref[half, row].astype(f32) + added
            merged = jnp.concatenate([merged, jnp.zeros((unit, lanes - width), f32)], axis=-1)
            halves[half, into, :] = merged.astype(bf16)
            strips[0, half, from_row, :] = pltpu.roll(merged, lanes - width, 1)[:, lanes - 128:].astype(bf16)
            strips[1, half, from_row, :] = pltpu.roll(merged, width, 1)[:, lanes - 128:].astype(bf16)

    def sideways(way):
        other = lax.rem(coil + (1, coils - 1)[way], coils)
        return pltpu.make_async_remote_copy(
            src_ref=strips.at[way], dst_ref=borders.at[way], send_sem=col_sent.at[way], recv_sem=col_got.at[way],
            device_id={"coil": other}, device_id_type=mesh_id)

    def upright(way, half):
        other = lax.rem(space + (1, spaces - 1)[way], spaces)
        source = (rows, HALO)[way] * unit
        target = (0, HALO + rows)[way] * unit
        return pltpu.make_async_remote_copy(
            src_ref=halves.at[half, pl.ds(source, HALO * unit)],
            dst_ref=halves.at[half, pl.ds(target, HALO * unit)],
            send_sem=row_sent.at[way, half], recv_sem=row_got.at[way, half],
            device_id={"space": other}, device_id_type=mesh_id)

    has_left, has_right = coil > 0, coil < coils - 1
    has_above, has_below = space > 0, space < spaces - 1

    @pl.when(has_right)
    def _():
        sideways(0).start()

    @pl.when(has_left)
    def _():
        sideways(1).start()

    edge = lax.broadcasted_iota(jnp.int32, (1, 128), 1)

    @pl.when(has_left)
    def _():
        sideways(0).wait_recv()

        @pl.loop(0, rows)
        def _(row):
            into = pl.ds(pl.multiple_of((row + HALO) * unit, unit), unit)
            from_row = pl.ds(pl.multiple_of(row * unit, unit), unit)
            for half in range(2):
                own = halves[half, into, lanes - 128:].astype(f32)
                new = borders[0, half, from_row, :].astype(f32)
                halves[half, into, lanes - 128:] = jnp.where(edge >= 128 - HALO, new, own).astype(bf16)

    @pl.when(has_right)
    def _():
        sideways(1).wait_recv()
        first = width % 128

        @pl.loop(0, rows)
        def _(row):
            into = pl.ds(pl.multiple_of((row + HALO) * unit, unit), unit)
            from_row = pl.ds(pl.multiple_of(row * unit, unit), unit)
            for half in range(2):
                own = halves[half, into, lanes - 128:].astype(f32)
                new = borders[1, half, from_row, :].astype(f32)
                inside = (edge >= first) & (edge < first + HALO)
                halves[half, into, lanes - 128:] = jnp.where(inside, new, own).astype(bf16)

    for half in range(2):
        @pl.when(has_below)
        def _(half=half):
            upright(0, half).start()

        @pl.when(has_above)
        def _(half=half):
            upright(1, half).start()

    for half in range(2):
        @pl.when(has_below)
        def _(half=half):
            upright(0, half).wait_send()
            upright(1, half).wait_recv()

        @pl.when(has_above)
        def _(half=half):
            upright(1, half).wait_send()
            upright(0, half).wait_recv()

    @pl.when(has_right)
    def _():
        sideways(0).wait_send()

    @pl.when(has_left)
    def _():
        sideways(1).wait_send()

    lane = lax.broadcasted_iota(jnp.int32, (1, lanes), 1)
    column = jnp.where(lane >= lanes - HALO, lane - lanes, lane) + col_start
    column_ok = jnp.where((column >= 0) & (column < total_cols), 1.0, 0.0)
    for layer in range(layers):
        source, target = layer % 2, 1 - layer % 2

        @pl.loop(0, halves.shape[1] // (2 * unit))
        def _(pair, source=source):
            for one in range(2):
                index = 2 * pair + one
                at = pl.ds(pl.multiple_of(index * unit, unit), unit)
                line = halves[source, at, :]
                wide = line.astype(f32)
                moved = (pltpu.roll(wide, 1, 1).astype(bf16), line, pltpu.roll(wide, lanes - 1, 1).astype(bf16))
                for c in range(3):
                    shifted[pl.ds(pl.multiple_of((3 * index + c) * unit, unit), unit), :] = moved[c]

        left = halo_rows - 2 * layer - 2
        steps = -(-left // BLOCK)

        @pl.loop(0, steps)
        def _(index, layer=layer, target=target):
            start = layer + index * BLOCK
            inside = pl.ds(pl.multiple_of(start * 3 * unit, 3 * unit), (BLOCK + 2) * 3 * unit)
            raw = jnp.dot(weight_ref[layer], shifted[inside, :], preferred_element_type=f32)
            hidden = jnp.maximum(raw + bias_ref[layer], 0.0)
            step = lax.broadcasted_iota(jnp.int32, (BLOCK * unit, 1), 0) // unit
            row = step + (start + 1 + row_start)
            row_ok = jnp.where((row >= 0) & (row < total_rows), 1.0, 0.0)
            hidden = (hidden * (row_ok * column_ok)).astype(bf16)
            update = jnp.dot(mixer_ref[layer], hidden, preferred_element_type=f32)
            at = pl.ds(pl.multiple_of((start + 1) * unit, unit), BLOCK * unit)
            halves[target, at, :] = (halves[target, at, :].astype(f32) + update).astype(bf16)

    for half in range(2):
        out_ref[half] = halves[half, HALO * unit:(HALO + rows) * unit, 0:width]


def couple(cells, gradient, inject, kernels, biases, mixers, total_rows, total_cols):
    _, rows, unit, width = cells.shape
    positions = gradient.shape[1]
    half = unit // positions
    layers = kernels.shape[0]
    lanes = -(-(width + 2 * HALO) // 128) * 128
    spaces, coils = lax.axis_size("space"), lax.axis_size("coil")
    held = rows + 2 * HALO + 8
    bias = jnp.tile(biases, (1, positions * BLOCK))[:, :, None]
    spread = jnp.tile(jnp.transpose(inject.reshape(2, half, 2), (0, 2, 1)), (1, 1, positions))[..., None]
    vmem = pl.BlockSpec(memory_space=pltpu.VMEM)
    dma = pltpu.SemaphoreType.DMA
    out = pl.pallas_call(
        functools.partial(couplings_body, layers, rows, width, lanes, total_rows, total_cols, unit, spaces, coils),
        out_shape=jax.ShapeDtypeStruct((2, rows * unit, width), jnp.bfloat16),
        in_specs=[vmem] * 6,
        out_specs=vmem,
        scratch_shapes=[
            pltpu.VMEM((2, held * unit, lanes), jnp.bfloat16),
            pltpu.VMEM((3 * held * unit, lanes), jnp.bfloat16),
            pltpu.VMEM((2, 2, rows * unit, 128), jnp.bfloat16),
            pltpu.VMEM((2, 2, rows * unit, 128), jnp.bfloat16),
            dma((2,)), dma((2,)), dma((2, 2)), dma((2, 2)),
        ],
        compiler_params=pltpu.CompilerParams(
            collective_id=1, has_side_effects=True, vmem_limit_bytes=56 * 1024 * 1024),
    )(cells, gradient, spread, coupling_weights(kernels), mixer_weights(mixers), bias)
    out = out.reshape(2, rows, positions, half, width)
    return jnp.transpose(out, (0, 3, 2, 1, 4)).reshape(2 * half, positions, rows, width)


def per_device(state, sens, kdata, mask, inject, kernels, biases, mixers):
    npar = sens.shape[4]
    npe = kdata.shape[4]
    gradient, cells = find_gradient(state, sens, kdata, mask)
    new_state = couple(cells, gradient, inject, kernels, biases, mixers, npe, npar)
    return (new_state, gradient)


def solution(mesh):
    return jax.shard_map(
        per_device,
        mesh=mesh,
        in_specs=(
            P(None, None, "space", "coil"),
            P(None, "coil", None, "space", None),
            P(None, "coil", None, "space", None),
            P("space", None),
            P(),
            P(),
            P(),
            P(),
        ),
        out_specs=(P(None, None, "space", "coil"), P(None, None, "space", "coil")),
        check_vma=False,
    )
```

```python
import functools
import math

import jax
import jax.numpy as jnp
from jax import lax
from jax.experimental import pallas as pl
from jax.experimental.pallas import tpu as pltpu
from jax.sharding import PartitionSpec as P


def dft_table(length):
    inner = 32
    column = lax.iota(jnp.int32, length)[None, :]
    fine = lax.iota(jnp.int32, inner)[:, None] * column % length
    coarse = (lax.iota(jnp.int32, length // inner)[:, None] * inner) * column % length
    unit = 2.0 * math.pi / length
    fine = fine.astype(jnp.float32) * unit
    coarse = coarse.astype(jnp.float32) * unit
    scale = 1.0 / math.sqrt(length)
    return (
        jnp.stack([jnp.cos(fine), jnp.sin(fine)]),
        jnp.stack([jnp.cos(coarse), jnp.sin(coarse)]) * scale,
    )


def fill_table(table, fine_ref, coarse_ref):
    inner = fine_ref.shape[1]

    @pl.loop(0, coarse_ref.shape[1])
    def _(a):
        cos, sin = coarse_ref[0, pl.ds(a, 1), :], coarse_ref[1, pl.ds(a, 1), :]
        at = pl.ds(pl.multiple_of(a * inner, inner), inner)
        table[0, at, :] = (cos * fine_ref[0] - sin * fine_ref[1]).astype(jnp.bfloat16)
        table[1, at, :] = (sin * fine_ref[0] + cos * fine_ref[1]).astype(jnp.bfloat16)


def gradient_body(spaces, coils, estimate_ref, mask_ref, par_fine, par_coarse, pe_fine, pe_coarse,
                  sens_hbm, kdata_hbm, state_hbm, out_ref, cells_hbm,
                  sens_ref, kdata_ref, state_ref, cells_ref, par_ref, pe_ref,
                  sens_in, kdata_in, state_in, cells_out,
                  seen, whole, send_out, got_out, send_back, got_back, total, part, parts,
                  seen_sent, seen_got, out_sent, out_got, back_sent, back_got, part_sent, part_got):
    space = lax.axis_index("space")
    coil = lax.axis_index("coil")
    f32, bf16 = jnp.float32, jnp.bfloat16
    width = estimate_ref.shape[2]
    count, positions, rows, npar = sens_ref.shape[1:]
    held, npe = kdata_ref.shape[3:]
    sites = positions * rows
    lines = positions * held

    fetch_kdata = pltpu.make_async_copy(kdata_hbm, kdata_ref, kdata_in)
    fetch_state = pltpu.make_async_copy(state_hbm, state_ref, state_in)
    store_cells = pltpu.make_async_copy(cells_ref, cells_hbm, cells_out)

    def fetch_sens(c):
        return pltpu.make_async_copy(sens_hbm.at[:, c], sens_ref.at[:, c], sens_in.at[c])

    @pl.loop(0, count)
    def _(c):
        fetch_sens(c).start()

    fetch_state.start()
    fetch_kdata.start()

    barrier = pltpu.get_barrier_semaphore()

    @pl.loop(1, spaces)
    def _(offset):
        pl.semaphore_signal(barrier, inc=1, device_id={"space": lax.rem(space + offset, spaces)},
                            device_id_type=pl.DeviceIdType.MESH)

    for offset in range(1, coils):
        pl.semaphore_signal(barrier, inc=1, device_id={"coil": lax.rem(coil + offset, coils)},
                            device_id_type=pl.DeviceIdType.MESH)
    pl.semaphore_wait(barrier, spaces + coils - 2)

    def to_coil(source, target, offset, sent, got):
        return pltpu.make_async_remote_copy(
            src_ref=source, dst_ref=target, send_sem=sent.at[offset], recv_sem=got.at[offset],
            device_id={"coil": lax.rem(coil + offset, coils)}, device_id_type=pl.DeviceIdType.MESH)

    def to_space(buffer, target, c, offset, sent, got):
        other = lax.rem(space + offset, spaces)
        return pltpu.make_async_remote_copy(
            src_ref=buffer.at[c, other], dst_ref=target.at[c, space], send_sem=sent.at[c], recv_sem=got.at[c],
            device_id={"space": other}, device_id_type=pl.DeviceIdType.MESH)

    def all_of(buffer, c, sem):
        span = buffer.at[c, pl.ds(0, spaces - 1)]
        pltpu.make_async_copy(span, span, sem.at[c]).wait()

    for offset in range(1, coils):
        to_coil(estimate_ref, seen.at[coil], offset, seen_sent, seen_got).start()
    seen[coil] = estimate_ref[...]
    fill_table(par_ref, par_fine, par_coarse)
    for offset in range(1, coils):
        to_coil(estimate_ref, seen.at[coil], offset, seen_sent, seen_got).wait()
    for part_of in range(2):
        whole[part_of] = jnp.concatenate([seen[j, part_of].astype(f32) for j in range(coils)], axis=-1)

    @pl.loop(0, count)
    def _(c):
        fetch_sens(c).wait()
        profile_real = sens_ref[0, c].reshape(sites, npar)
        profile_imag = sens_ref[1, c].reshape(sites, npar)
        real = profile_real * whole[0] - profile_imag * whole[1]
        imag = profile_real * whole[1] + profile_imag * whole[0]
        plain = jnp.concatenate([real, imag], axis=0).astype(bf16)
        turned = jnp.concatenate([imag, -real], axis=0).astype(bf16)
        along = (((1,), (1,)), ((), ()))
        spectrum = lax.dot_general(par_ref[0], plain, along, preferred_element_type=f32)
        spectrum += lax.dot_general(par_ref[1], turned, along, preferred_element_type=f32)
        send_out[c] = spectrum.reshape(spaces, held, 2 * sites).astype(bf16)

        @pl.loop(1, spaces)
        def _(offset):
            to_space(send_out, got_out, c, offset, out_sent, out_got).start()

        got_out[c, space] = send_out[c, space]

    fill_table(pe_ref, pe_fine, pe_coarse)
    fetch_state.wait()
    half = state_ref.shape[0] // 2
    group = 16

    @pl.loop(0, rows // group)
    def _(g):
        at = pl.ds(pl.multiple_of(g * group, group), group)
        for side in range(2):
            for position in range(positions):
                cells = state_ref[side * half:(side + 1) * half, position, at, :].astype(f32)
                cells_ref[side, at, position * half:(position + 1) * half, :] = jnp.swapaxes(cells, 0, 1).astype(bf16)

    store_cells.start()
    fetch_kdata.wait()

    @pl.loop(0, count)
    def _(c):
        all_of(got_out, c, out_got)
        blocks = [got_out[c, s].astype(f32) for s in range(spaces)]
        grid = [
            jnp.concatenate([block[:, k * rows:(k + 1) * rows] for block in blocks], axis=-1)
            for k in range(2 * positions)
        ]
        real = jnp.concatenate(grid[:positions], axis=0)
        imag = jnp.concatenate(grid[positions:], axis=0)
        plain = jnp.concatenate([real, imag], axis=0).astype(bf16)
        turned = jnp.concatenate([imag, -real], axis=0).astype(bf16)
        full = jnp.dot(plain, pe_ref[0], preferred_element_type=f32)
        full += jnp.dot(turned, pe_ref[1], preferred_element_type=f32)
        sampled = jnp.concatenate([mask_ref[...].astype(f32)] * positions, axis=0)
        real = sampled * (full[:lines] - kdata_ref[0, c].reshape(lines, npe))
        imag = sampled * (full[lines:] - kdata_ref[1, c].reshape(lines, npe))
        plain = jnp.concatenate([real, imag], axis=0).astype(bf16)
        turned = jnp.concatenate([-imag, real], axis=0).astype(bf16)
        back = jnp.dot(plain, pe_ref[0], preferred_element_type=f32)
        back += jnp.dot(turned, pe_ref[1], preferred_element_type=f32)
        for s in range(spaces):
            send_back[c, s] = jnp.concatenate(
                [back[k * held:(k + 1) * held, s * rows:(s + 1) * rows] for k in range(2 * positions)], axis=-1
            ).astype(bf16)

        @pl.loop(1, spaces)
        def _(offset):
            to_space(send_back, got_back, c, offset, back_sent, back_got).start()

        got_back[c, space] = send_back[c, space]

    total[...] = jnp.zeros_like(total)

    @pl.loop(0, count)
    def _(c):
        all_of(got_back, c, back_got)
        plain = got_back[c].astype(f32).reshape(npar, 2 * sites)
        turned = jnp.concatenate([-plain[:, sites:], plain[:, :sites]], axis=-1).astype(bf16)
        along = (((0,), (0,)), ((), ()))
        image = lax.dot_general(plain.astype(bf16), par_ref[0], along, preferred_element_type=f32)
        image += lax.dot_general(turned, par_ref[1], along, preferred_element_type=f32)
        real, imag = image[:sites], image[sites:]
        profile_real = sens_ref[0, c].reshape(sites, npar)
        profile_imag = sens_ref[1, c].reshape(sites, npar)
        total[0] += profile_real * real + profile_imag * imag
        total[1] += profile_real * imag - profile_imag * real

    for j in range(coils):
        for part_of in range(2):
            part[j, part_of] = total[part_of, :, j * width:(j + 1) * width].astype(bf16)
    for offset in range(1, coils):
        to_coil(part.at[lax.rem(coil + offset, coils)], parts.at[coil], offset, part_sent, part_got).start()
    parts[coil] = part[coil]
    for offset in range(1, coils):
        to_coil(part.at[lax.rem(coil + offset, coils)], parts.at[coil], offset, part_sent, part_got).wait()
    result = parts[0].astype(f32)
    for j in range(1, coils):
        result += parts[j].astype(f32)
    out_ref[...] = result
    store_cells.wait()

    @pl.loop(0, count)
    def _(c):
        all_of(send_out, c, out_sent)
        all_of(send_back, c, back_sent)


def find_gradient(state, sens, kdata, mask):
    spaces, coils = lax.axis_size("space"), lax.axis_size("coil")
    _, positions, rows, width = state.shape
    count, npar = sens.shape[1], sens.shape[4]
    held, npe = kdata.shape[3:]
    sites = positions * rows
    bf16, f32 = jnp.bfloat16, jnp.float32
    vmem = pl.BlockSpec(memory_space=pltpu.VMEM)
    hbm = pl.BlockSpec(memory_space=pl.ANY)
    dma = pltpu.SemaphoreType.DMA
    message = pltpu.VMEM((count, spaces, held, 2 * sites), bf16)
    channels = state.shape[0]
    result, cells = pl.pallas_call(
        functools.partial(gradient_body, spaces, coils),
        out_shape=(
            jax.ShapeDtypeStruct((2, sites, width), f32),
            jax.ShapeDtypeStruct((2, rows, positions * channels // 2, width), bf16),
        ),
        in_specs=[vmem] * 6 + [hbm] * 3,
        out_specs=(vmem, hbm),
        scratch_shapes=[
            pltpu.VMEM(sens.shape, f32),
            pltpu.VMEM(kdata.shape, f32),
            pltpu.VMEM(state.shape, bf16),
            pltpu.VMEM((2, rows, positions * channels // 2, width), bf16),
            pltpu.VMEM((2, npar, npar), bf16),
            pltpu.VMEM((2, npe, npe), bf16),
            dma((count,)), dma, dma, dma,
            pltpu.VMEM((coils, 2, sites, width), bf16),
            pltpu.VMEM((2, sites, npar), f32),
            message, message, message, message,
            pltpu.VMEM((2, sites, npar), f32),
            pltpu.VMEM((coils, 2, sites, width), bf16),
            pltpu.VMEM((coils, 2, sites, width), bf16),
            dma((coils,)), dma((coils,)), dma((count,)), dma((count,)),
            dma((count,)), dma((count,)), dma((coils,)), dma((coils,)),
        ],
        compiler_params=pltpu.CompilerParams(
            collective_id=0, has_side_effects=True, vmem_limit_bytes=60 * 1024 * 1024),
    )(state[0:2].reshape(2, sites, width), mask, *dft_table(npar), *dft_table(npe), sens, kdata, state)
    return result.reshape(2, positions, rows, width), cells


HALO = 4
BLOCK = 6


def coupling_weights(kernels):
    layers, _, outs, ins = kernels.shape
    taps = kernels.reshape(layers, 3, 3, 3, outs, ins)
    rows = []
    for out_pos in range(2):
        rows.append(jnp.concatenate([taps[:, in_pos - out_pos + 1] for in_pos in range(2)], axis=-1))
    mixed = jnp.concatenate(rows, axis=-2)
    strip = jnp.concatenate([mixed[:, b, c] for b in range(3) for c in range(3)], axis=-1)
    unit = 6 * ins
    bands = [
        jnp.pad(strip, ((0, 0), (0, 0), (unit * x, unit * (BLOCK - 1 - x)))) for x in range(BLOCK)
    ]
    return jnp.concatenate(bands, axis=-2)


def mixer_weights(mixers):
    ins = mixers.shape[2]
    times = 2 * BLOCK
    bands = [jnp.pad(mixers, ((0, 0), (0, 0), (ins * x, ins * (times - 1 - x)))) for x in range(times)]
    return jnp.concatenate(bands, axis=-2)


def couplings_body(layers, rows, width, lanes, total_rows, total_cols, unit, spaces, coils,
                   cells_ref, gradient_ref, inject_ref, weight_ref, mixer_ref, bias_ref, out_ref,
                   halves, shifted, strips, borders, col_sent, col_got, row_sent, row_got):
    f32, bf16 = jnp.float32, jnp.bfloat16
    mesh_id = pl.DeviceIdType.MESH
    space = lax.axis_index("space")
    coil = lax.axis_index("coil")
    positions = gradient_ref.shape[1]
    halo_rows = rows + 2 * HALO
    row_start = space * rows - HALO
    col_start = coil * width

    barrier = pltpu.get_barrier_semaphore()
    for step in (1, -1):
        pl.semaphore_signal(barrier, inc=1, device_id={"coil": lax.rem(coil + step + coils, coils)}, device_id_type=mesh_id)
        pl.semaphore_signal(barrier, inc=1, device_id={"space": lax.rem(space + step + spaces, spaces)}, device_id_type=mesh_id)
    pl.semaphore_wait(barrier, 4)

    for half in range(2):
        spare = (halves.shape[1] - halo_rows * unit, lanes)
        halves[half, halo_rows * unit:, :] = jnp.zeros(spare, bf16)

        @pl.when(space == 0)
        def _(half=half):
            halves[half, 0:HALO * unit, :] = jnp.zeros((HALO * unit, lanes), bf16)

        @pl.when(space == spaces - 1)
        def _(half=half):
            halves[half, (HALO + rows) * unit:halo_rows * unit, :] = jnp.zeros((HALO * unit, lanes), bf16)

    @pl.loop(0, rows)
    def _(row):
        lines = [
            jnp.concatenate(
                [
                    jnp.broadcast_to(gradient_ref[g, p, pl.ds(row, 1), :], (unit // positions, width))
                    for p in range(positions)
                ],
                axis=0,
            )
            for g in range(2)
        ]
        from_row = pl.ds(pl.multiple_of(row * unit, unit), unit)
        into = pl.ds(pl.multiple_of((row + HALO) * unit, unit), unit)
        for half in range(2):
            added = inject_ref[half, 0] * lines[0] + inject_ref[half, 1] * lines[1]
            merged = cells_ref[half, row].astype(f32) + added
            merged = jnp.concatenate([merged, jnp.zeros((unit, lanes - width), f32)], axis=-1)
            halves[half, into, :] = merged.astype(bf16)
            strips[0, half, from_row, :] = pltpu.roll(merged, lanes - width, 1)[:, lanes - 128:].astype(bf16)
            strips[1, half, from_row, :] = pltpu.roll(merged, width, 1)[:, lanes - 128:].astype(bf16)

    def sideways(way):
        other = lax.rem(coil + (1, coils - 1)[way], coils)
        return pltpu.make_async_remote_copy(
            src_ref=strips.at[way], dst_ref=borders.at[way], send_sem=col_sent.at[way], recv_sem=col_got.at[way],
            device_id={"coil": other}, device_id_type=mesh_id)

    def upright(way, half):
        other = lax.rem(space + (1, spaces - 1)[way], spaces)
        source = (rows, HALO)[way] * unit
        target = (0, HALO + rows)[way] * unit
        return pltpu.make_async_remote_copy(
            src_ref=halves.at[half, pl.ds(source, HALO * unit)],
            dst_ref=halves.at[half, pl.ds(target, HALO * unit)],
            send_sem=row_sent.at[way, half], recv_sem=row_got.at[way, half],
            device_id={"space": other}, device_id_type=mesh_id)

    has_left, has_right = coil > 0, coil < coils - 1
    has_above, has_below = space > 0, space < spaces - 1

    @pl.when(has_right)
    def _():
        sideways(0).start()

    @pl.when(has_left)
    def _():
        sideways(1).start()

    edge = lax.broadcasted_iota(jnp.int32, (1, 128), 1)

    @pl.when(has_left)
    def _():
        sideways(0).wait_recv()

        @pl.loop(0, rows)
        def _(row):
            into = pl.ds(pl.multiple_of((row + HALO) * unit, unit), unit)
            from_row = pl.ds(pl.multiple_of(row * unit, unit), unit)
            for half in range(2):
                own = halves[half, into, lanes - 128:].astype(f32)
                new = borders[0, half, from_row, :].astype(f32)
                halves[half, into, lanes - 128:] = jnp.where(edge >= 128 - HALO, new, own).astype(bf16)

    @pl.when(has_right)
    def _():
        sideways(1).wait_recv()
        first = width % 128

        @pl.loop(0, rows)
        def _(row):
            into = pl.ds(pl.multiple_of((row + HALO) * unit, unit), unit)
            from_row = pl.ds(pl.multiple_of(row * unit, unit), unit)
            for half in range(2):
                own = halves[half, into, lanes - 128:].astype(f32)
                new = borders[1, half, from_row, :].astype(f32)
                inside = (edge >= first) & (edge < first + HALO)
                halves[half, into, lanes - 128:] = jnp.where(inside, new, own).astype(bf16)

    for half in range(2):
        @pl.when(has_below)
        def _(half=half):
            upright(0, half).start()

        @pl.when(has_above)
        def _(half=half):
            upright(1, half).start()

    for half in range(2):
        @pl.when(has_below)
        def _(half=half):
            upright(0, half).wait_send()
            upright(1, half).wait_recv()

        @pl.when(has_above)
        def _(half=half):
            upright(1, half).wait_send()
            upright(0, half).wait_recv()

    @pl.when(has_right)
    def _():
        sideways(0).wait_send()

    @pl.when(has_left)
    def _():
        sideways(1).wait_send()

    lane = lax.broadcasted_iota(jnp.int32, (1, lanes), 1)
    column = jnp.where(lane >= lanes - HALO, lane - lanes, lane) + col_start
    column_ok = jnp.where((column >= 0) & (column < total_cols), 1.0, 0.0)
    for layer in range(layers):
        source, target = layer % 2, 1 - layer % 2

        @pl.loop(0, halves.shape[1] // (4 * unit))
        def _(pair, source=source):
            for one in range(4):
                index = 4 * pair + one
                at = pl.ds(pl.multiple_of(index * unit, unit), unit)
                line = halves[source, at, :]
                wide = line.astype(f32)
                moved = (pltpu.roll(wide, 1, 1).astype(bf16), line, pltpu.roll(wide, lanes - 1, 1).astype(bf16))
                for c in range(3):
                    shifted[pl.ds(pl.multiple_of((3 * index + c) * unit, unit), unit), :] = moved[c]

        left = halo_rows - 2 * layer - 2
        steps = -(-left // BLOCK)

        for index in range(steps):
            start = layer + index * BLOCK
            inside = pl.ds(start * 3 * unit, (BLOCK + 2) * 3 * unit)
            raw = jnp.dot(weight_ref[layer], shifted[inside, :], preferred_element_type=f32)
            hidden = jnp.maximum(raw + bias_ref[layer], 0.0)
            step = lax.broadcasted_iota(jnp.int32, (BLOCK * unit, 1), 0) // unit
            row = step + (start + 1 + row_start)
            row_ok = jnp.where((row >= 0) & (row < total_rows), 1.0, 0.0)
            hidden = (hidden * (row_ok * column_ok)).astype(bf16)
            update = jnp.dot(mixer_ref[layer], hidden, preferred_element_type=f32)
            at = pl.ds((start + 1) * unit, BLOCK * unit)
            halves[target, at, :] = (halves[target, at, :].astype(f32) + update).astype(bf16)

    for half in range(2):
        out_ref[half] = halves[half, HALO * unit:(HALO + rows) * unit, 0:width]


def couple(cells, gradient, inject, kernels, biases, mixers, total_rows, total_cols):
    _, rows, unit, width = cells.shape
    positions = gradient.shape[1]
    half = unit // positions
    layers = kernels.shape[0]
    lanes = -(-(width + 2 * HALO) // 128) * 128
    spaces, coils = lax.axis_size("space"), lax.axis_size("coil")
    held = rows + 2 * HALO + 8
    bias = jnp.tile(biases, (1, positions * BLOCK))[:, :, None]
    spread = jnp.tile(jnp.transpose(inject.reshape(2, half, 2), (0, 2, 1)), (1, 1, positions))[..., None]
    vmem = pl.BlockSpec(memory_space=pltpu.VMEM)
    dma = pltpu.SemaphoreType.DMA
    out = pl.pallas_call(
        functools.partial(couplings_body, layers, rows, width, lanes, total_rows, total_cols, unit, spaces, coils),
        out_shape=jax.ShapeDtypeStruct((2, rows * unit, width), jnp.bfloat16),
        in_specs=[vmem] * 6,
        out_specs=vmem,
        scratch_shapes=[
            pltpu.VMEM((2, held * unit, lanes), jnp.bfloat16),
            pltpu.VMEM((3 * held * unit, lanes), jnp.bfloat16),
            pltpu.VMEM((2, 2, rows * unit, 128), jnp.bfloat16),
            pltpu.VMEM((2, 2, rows * unit, 128), jnp.bfloat16),
            dma((2,)), dma((2,)), dma((2, 2)), dma((2, 2)),
        ],
        compiler_params=pltpu.CompilerParams(
            collective_id=1, has_side_effects=True, vmem_limit_bytes=56 * 1024 * 1024),
    )(cells, gradient, spread, coupling_weights(kernels), mixer_weights(mixers), bias)
    out = out.reshape(2, rows, positions, half, width)
    return jnp.transpose(out, (0, 3, 2, 1, 4)).reshape(2 * half, positions, rows, width)


def per_device(state, sens, kdata, mask, inject, kernels, biases, mixers):
    npar = sens.shape[4]
    npe = kdata.shape[4]
    gradient, cells = find_gradient(state, sens, kdata, mask)
    new_state = couple(cells, gradient, inject, kernels, biases, mixers, npe, npar)
    return (new_state, gradient)


def solution(mesh):
    return jax.shard_map(
        per_device,
        mesh=mesh,
        in_specs=(
            P(None, None, "space", "coil"),
            P(None, "coil", None, "space", None),
            P(None, "coil", None, "space", None),
            P("space", None),
            P(),
            P(),
            P(),
            P(),
        ),
        out_specs=(P(None, None, "space", "coil"), P(None, None, "space", "coil")),
        check_vma=False,
    )
```

```python
import functools
import math

import jax
import jax.numpy as jnp
import numpy as np
from jax import lax
from jax.experimental import pallas as pl
from jax.experimental.pallas import tpu as pltpu
from jax.sharding import PartitionSpec as P


def dft_table(length):
    inner = 32
    column = np.arange(length)[None, :]
    fine = np.arange(inner)[:, None] * column % length * (2.0 * math.pi / length)
    coarse = np.arange(0, length, inner)[:, None] * column % length * (2.0 * math.pi / length)
    scale = 1.0 / math.sqrt(length)
    return (
        jnp.asarray(np.stack([np.cos(fine), np.sin(fine)]).astype(np.float32)),
        jnp.asarray((np.stack([np.cos(coarse), np.sin(coarse)]) * scale).astype(np.float32)),
    )


def fill_table(table, fine_ref, coarse_ref):
    inner = fine_ref.shape[1]

    @pl.loop(0, coarse_ref.shape[1])
    def _(a):
        cos, sin = coarse_ref[0, pl.ds(a, 1), :], coarse_ref[1, pl.ds(a, 1), :]
        at = pl.ds(pl.multiple_of(a * inner, inner), inner)
        table[0, at, :] = (cos * fine_ref[0] - sin * fine_ref[1]).astype(jnp.bfloat16)
        table[1, at, :] = (sin * fine_ref[0] + cos * fine_ref[1]).astype(jnp.bfloat16)


def gradient_body(spaces, coils, estimate_ref, mask_ref, par_fine, par_coarse, pe_fine, pe_coarse,
                  sens_hbm, kdata_hbm, state_hbm, out_ref, cells_hbm,
                  sens_ref, kdata_ref, state_ref, cells_ref, par_ref, pe_ref,
                  sens_in, kdata_in, state_in, cells_out,
                  seen, whole, send_out, got_out, send_back, got_back, total, part, parts,
                  seen_sent, seen_got, out_sent, out_got, back_sent, back_got, part_sent, part_got):
    space = lax.axis_index("space")
    coil = lax.axis_index("coil")
    f32, bf16 = jnp.float32, jnp.bfloat16
    width = estimate_ref.shape[2]
    count, positions, rows, npar = sens_ref.shape[1:]
    held, npe = kdata_ref.shape[3:]
    sites = positions * rows
    lines = positions * held

    fetch_kdata = pltpu.make_async_copy(kdata_hbm, kdata_ref, kdata_in)
    fetch_state = pltpu.make_async_copy(state_hbm, state_ref, state_in)
    store_cells = pltpu.make_async_copy(cells_ref, cells_hbm, cells_out)

    def fetch_sens(c):
        return pltpu.make_async_copy(sens_hbm.at[:, c], sens_ref.at[:, c], sens_in.at[c])

    @pl.loop(0, count)
    def _(c):
        fetch_sens(c).start()

    fetch_state.start()
    fetch_kdata.start()

    barrier = pltpu.get_barrier_semaphore()

    @pl.loop(1, spaces)
    def _(offset):
        pl.semaphore_signal(barrier, inc=1, device_id={"space": lax.rem(space + offset, spaces)},
                            device_id_type=pl.DeviceIdType.MESH)

    for offset in range(1, coils):
        pl.semaphore_signal(barrier, inc=1, device_id={"coil": lax.rem(coil + offset, coils)},
                            device_id_type=pl.DeviceIdType.MESH)
    pl.semaphore_wait(barrier, spaces + coils - 2)

    def to_coil(source, target, offset, sent, got):
        return pltpu.make_async_remote_copy(
            src_ref=source, dst_ref=target, send_sem=sent.at[offset], recv_sem=got.at[offset],
            device_id={"coil": lax.rem(coil + offset, coils)}, device_id_type=pl.DeviceIdType.MESH)

    def to_space(buffer, target, c, offset, sent, got):
        other = lax.rem(space + offset, spaces)
        return pltpu.make_async_remote_copy(
            src_ref=buffer.at[c, other], dst_ref=target.at[c, space], send_sem=sent.at[c], recv_sem=got.at[c],
            device_id={"space": other}, device_id_type=pl.DeviceIdType.MESH)

    def all_of(buffer, c, sem):
        span = buffer.at[c, pl.ds(0, spaces - 1)]
        pltpu.make_async_copy(span, span, sem.at[c]).wait()

    for offset in range(1, coils):
        to_coil(estimate_ref, seen.at[coil], offset, seen_sent, seen_got).start()
    seen[coil] = estimate_ref[...]
    fill_table(par_ref, par_fine, par_coarse)
    for offset in range(1, coils):
        to_coil(estimate_ref, seen.at[coil], offset, seen_sent, seen_got).wait()
    for part_of in range(2):
        whole[part_of] = jnp.concatenate([seen[j, part_of].astype(f32) for j in range(coils)], axis=-1)

    @pl.loop(0, count)
    def _(c):
        fetch_sens(c).wait()
        profile_real = sens_ref[0, c].reshape(sites, npar)
        profile_imag = sens_ref[1, c].reshape(sites, npar)
        real = profile_real * whole[0] - profile_imag * whole[1]
        imag = profile_real * whole[1] + profile_imag * whole[0]
        plain = jnp.concatenate([real, imag], axis=0).astype(bf16)
        turned = jnp.concatenate([imag, -real], axis=0).astype(bf16)
        along = (((1,), (1,)), ((), ()))
        spectrum = lax.dot_general(par_ref[0], plain, along, preferred_element_type=f32)
        spectrum += lax.dot_general(par_ref[1], turned, along, preferred_element_type=f32)
        send_out[c] = spectrum.reshape(spaces, held, 2 * sites).astype(bf16)

        @pl.loop(1, spaces)
        def _(offset):
            to_space(send_out, got_out, c, offset, out_sent, out_got).start()

        got_out[c, space] = send_out[c, space]

    fill_table(pe_ref, pe_fine, pe_coarse)
    fetch_state.wait()
    half = state_ref.shape[0] // 2
    group = 16

    @pl.loop(0, rows // group)
    def _(g):
        at = pl.ds(pl.multiple_of(g * group, group), group)
        for side in range(2):
            for position in range(positions):
                cells = state_ref[side * half:(side + 1) * half, position, at, :].astype(f32)
                cells_ref[side, at, position * half:(position + 1) * half, :] = jnp.swapaxes(cells, 0, 1).astype(bf16)

    store_cells.start()
    fetch_kdata.wait()

    @pl.loop(0, count)
    def _(c):
        all_of(got_out, c, out_got)
        blocks = [got_out[c, s].astype(f32) for s in range(spaces)]
        grid = [
            jnp.concatenate([block[:, k * rows:(k + 1) * rows] for block in blocks], axis=-1)
            for k in range(2 * positions)
        ]
        real = jnp.concatenate(grid[:positions], axis=0)
        imag = jnp.concatenate(grid[positions:], axis=0)
        plain = jnp.concatenate([real, imag], axis=0).astype(bf16)
        turned = jnp.concatenate([imag, -real], axis=0).astype(bf16)
        full = jnp.dot(plain, pe_ref[0], preferred_element_type=f32)
        full += jnp.dot(turned, pe_ref[1], preferred_element_type=f32)
        sampled = jnp.concatenate([mask_ref[...].astype(f32)] * positions, axis=0)
        real = sampled * (full[:lines] - kdata_ref[0, c].reshape(lines, npe))
        imag = sampled * (full[lines:] - kdata_ref[1, c].reshape(lines, npe))
        plain = jnp.concatenate([real, imag], axis=0).astype(bf16)
        turned = jnp.concatenate([-imag, real], axis=0).astype(bf16)
        back = jnp.dot(plain, pe_ref[0], preferred_element_type=f32)
        back += jnp.dot(turned, pe_ref[1], preferred_element_type=f32)
        for s in range(spaces):
            send_back[c, s] = jnp.concatenate(
                [back[k * held:(k + 1) * held, s * rows:(s + 1) * rows] for k in range(2 * positions)], axis=-1
            ).astype(bf16)

        @pl.loop(1, spaces)
        def _(offset):
            to_space(send_back, got_back, c, offset, back_sent, back_got).start()

        got_back[c, space] = send_back[c, space]

    total[...] = jnp.zeros_like(total)

    @pl.loop(0, count)
    def _(c):
        all_of(got_back, c, back_got)
        plain = got_back[c].astype(f32).reshape(npar, 2 * sites)
        turned = jnp.concatenate([-plain[:, sites:], plain[:, :sites]], axis=-1).astype(bf16)
        along = (((0,), (0,)), ((), ()))
        image = lax.dot_general(plain.astype(bf16), par_ref[0], along, preferred_element_type=f32)
        image += lax.dot_general(turned, par_ref[1], along, preferred_element_type=f32)
        real, imag = image[:sites], image[sites:]
        profile_real = sens_ref[0, c].reshape(sites, npar)
        profile_imag = sens_ref[1, c].reshape(sites, npar)
        total[0] += profile_real * real + profile_imag * imag
        total[1] += profile_real * imag - profile_imag * real

    for j in range(coils):
        for part_of in range(2):
            part[j, part_of] = total[part_of, :, j * width:(j + 1) * width].astype(bf16)
    for offset in range(1, coils):
        to_coil(part.at[lax.rem(coil + offset, coils)], parts.at[coil], offset, part_sent, part_got).start()
    parts[coil] = part[coil]
    for offset in range(1, coils):
        to_coil(part.at[lax.rem(coil + offset, coils)], parts.at[coil], offset, part_sent, part_got).wait()
    result = parts[0].astype(f32)
    for j in range(1, coils):
        result += parts[j].astype(f32)
    out_ref[...] = result
    store_cells.wait()

    @pl.loop(0, count)
    def _(c):
        all_of(send_out, c, out_sent)
        all_of(send_back, c, back_sent)


def find_gradient(state, sens, kdata, mask):
    spaces, coils = lax.axis_size("space"), lax.axis_size("coil")
    _, positions, rows, width = state.shape
    count, npar = sens.shape[1], sens.shape[4]
    held, npe = kdata.shape[3:]
    sites = positions * rows
    bf16, f32 = jnp.bfloat16, jnp.float32
    vmem = pl.BlockSpec(memory_space=pltpu.VMEM)
    hbm = pl.BlockSpec(memory_space=pl.ANY)
    dma = pltpu.SemaphoreType.DMA
    message = pltpu.VMEM((count, spaces, held, 2 * sites), bf16)
    channels = state.shape[0]
    result, cells = pl.pallas_call(
        functools.partial(gradient_body, spaces, coils),
        out_shape=(
            jax.ShapeDtypeStruct((2, sites, width), f32),
            jax.ShapeDtypeStruct((2, rows, positions * channels // 2, width), bf16),
        ),
        in_specs=[vmem] * 6 + [hbm] * 3,
        out_specs=(vmem, hbm),
        scratch_shapes=[
            pltpu.VMEM(sens.shape, f32),
            pltpu.VMEM(kdata.shape, f32),
            pltpu.VMEM(state.shape, bf16),
            pltpu.VMEM((2, rows, positions * channels // 2, width), bf16),
            pltpu.VMEM((2, npar, npar), bf16),
            pltpu.VMEM((2, npe, npe), bf16),
            dma((count,)), dma, dma, dma,
            pltpu.VMEM((coils, 2, sites, width), bf16),
            pltpu.VMEM((2, sites, npar), f32),
            message, message, message, message,
            pltpu.VMEM((2, sites, npar), f32),
            pltpu.VMEM((coils, 2, sites, width), bf16),
            pltpu.VMEM((coils, 2, sites, width), bf16),
            dma((coils,)), dma((coils,)), dma((count,)), dma((count,)),
            dma((count,)), dma((count,)), dma((coils,)), dma((coils,)),
        ],
        compiler_params=pltpu.CompilerParams(
            collective_id=0, has_side_effects=True, vmem_limit_bytes=60 * 1024 * 1024),
    )(state[0:2].reshape(2, sites, width), mask, *dft_table(npar), *dft_table(npe), sens, kdata, state)
    return result.reshape(2, positions, rows, width), cells


HALO = 4
BLOCK = 6


def coupling_weights(kernels):
    layers, _, outs, ins = kernels.shape
    taps = kernels.reshape(layers, 3, 3, 3, outs, ins)
    rows = []
    for out_pos in range(2):
        rows.append(jnp.concatenate([taps[:, in_pos - out_pos + 1] for in_pos in range(2)], axis=-1))
    mixed = jnp.concatenate(rows, axis=-2)
    strip = jnp.concatenate([mixed[:, b, c] for b in range(3) for c in range(3)], axis=-1)
    unit = 6 * ins
    bands = [
        jnp.pad(strip, ((0, 0), (0, 0), (unit * x, unit * (BLOCK - 1 - x)))) for x in range(BLOCK)
    ]
    return jnp.concatenate(bands, axis=-2)


def mixer_weights(mixers):
    ins = mixers.shape[2]
    times = 2 * BLOCK
    bands = [jnp.pad(mixers, ((0, 0), (0, 0), (ins * x, ins * (times - 1 - x)))) for x in range(times)]
    return jnp.concatenate(bands, axis=-2)


def couplings_body(layers, rows, width, lanes, total_rows, total_cols, unit, spaces, coils,
                   cells_ref, gradient_ref, inject_ref, weight_ref, mixer_ref, bias_ref, out_ref,
                   halves, shifted, strips, borders, col_sent, col_got, row_sent, row_got):
    f32, bf16 = jnp.float32, jnp.bfloat16
    mesh_id = pl.DeviceIdType.MESH
    space = lax.axis_index("space")
    coil = lax.axis_index("coil")
    positions = gradient_ref.shape[1]
    halo_rows = rows + 2 * HALO
    row_start = space * rows - HALO
    col_start = coil * width

    barrier = pltpu.get_barrier_semaphore()
    for step in (1, -1):
        pl.semaphore_signal(barrier, inc=1, device_id={"coil": lax.rem(coil + step + coils, coils)}, device_id_type=mesh_id)
        pl.semaphore_signal(barrier, inc=1, device_id={"space": lax.rem(space + step + spaces, spaces)}, device_id_type=mesh_id)
    pl.semaphore_wait(barrier, 4)

    for half in range(2):
        spare = (halves.shape[1] - halo_rows * unit, lanes)
        halves[half, halo_rows * unit:, :] = jnp.zeros(spare, bf16)

        @pl.when(space == 0)
        def _(half=half):
            halves[half, 0:HALO * unit, :] = jnp.zeros((HALO * unit, lanes), bf16)

        @pl.when(space == spaces - 1)
        def _(half=half):
            halves[half, (HALO + rows) * unit:halo_rows * unit, :] = jnp.zeros((HALO * unit, lanes), bf16)

    @pl.loop(0, rows)
    def _(row):
        lines = [
            jnp.concatenate(
                [
                    jnp.broadcast_to(gradient_ref[g, p, pl.ds(row, 1), :], (unit // positions, width))
                    for p in range(positions)
                ],
                axis=0,
            )
            for g in range(2)
        ]
        from_row = pl.ds(pl.multiple_of(row * unit, unit), unit)
        into = pl.ds(pl.multiple_of((row + HALO) * unit, unit), unit)
        for half in range(2):
            added = inject_ref[half, 0] * lines[0] + inject_ref[half, 1] * lines[1]
            merged = cells_ref[half, row].astype(f32) + added
            merged = jnp.concatenate([merged, jnp.zeros((unit, lanes - width), f32)], axis=-1)
            halves[half, into, :] = merged.astype(bf16)
            strips[0, half, from_row, :] = pltpu.roll(merged, lanes - width, 1)[:, lanes - 128:].astype(bf16)
            strips[1, half, from_row, :] = pltpu.roll(merged, width, 1)[:, lanes - 128:].astype(bf16)

    def sideways(way):
        other = lax.rem(coil + (1, coils - 1)[way], coils)
        return pltpu.make_async_remote_copy(
            src_ref=strips.at[way], dst_ref=borders.at[way], send_sem=col_sent.at[way], recv_sem=col_got.at[way],
            device_id={"coil": other}, device_id_type=mesh_id)

    def upright(way, half):
        other = lax.rem(space + (1, spaces - 1)[way], spaces)
        source = (rows, HALO)[way] * unit
        target = (0, HALO + rows)[way] * unit
        return pltpu.make_async_remote_copy(
            src_ref=halves.at[half, pl.ds(source, HALO * unit)],
            dst_ref=halves.at[half, pl.ds(target, HALO * unit)],
            send_sem=row_sent.at[way, half], recv_sem=row_got.at[way, half],
            device_id={"space": other}, device_id_type=mesh_id)

    has_left, has_right = coil > 0, coil < coils - 1
    has_above, has_below = space > 0, space < spaces - 1

    @pl.when(has_right)
    def _():
        sideways(0).start()

    @pl.when(has_left)
    def _():
        sideways(1).start()

    edge = lax.broadcasted_iota(jnp.int32, (1, 128), 1)

    @pl.when(has_left)
    def _():
        sideways(0).wait_recv()

        @pl.loop(0, rows)
        def _(row):
            into = pl.ds(pl.multiple_of((row + HALO) * unit, unit), unit)
            from_row = pl.ds(pl.multiple_of(row * unit, unit), unit)
            for half in range(2):
                own = halves[half, into, lanes - 128:].astype(f32)
                new = borders[0, half, from_row, :].astype(f32)
                halves[half, into, lanes - 128:] = jnp.where(edge >= 128 - HALO, new, own).astype(bf16)

    @pl.when(has_right)
    def _():
        sideways(1).wait_recv()
        first = width % 128

        @pl.loop(0, rows)
        def _(row):
            into = pl.ds(pl.multiple_of((row + HALO) * unit, unit), unit)
            from_row = pl.ds(pl.multiple_of(row * unit, unit), unit)
            for half in range(2):
                own = halves[half, into, lanes - 128:].astype(f32)
                new = borders[1, half, from_row, :].astype(f32)
                inside = (edge >= first) & (edge < first + HALO)
                halves[half, into, lanes - 128:] = jnp.where(inside, new, own).astype(bf16)

    for half in range(2):
        @pl.when(has_below)
        def _(half=half):
            upright(0, half).start()

        @pl.when(has_above)
        def _(half=half):
            upright(1, half).start()

    for half in range(2):
        @pl.when(has_below)
        def _(half=half):
            upright(0, half).wait_send()
            upright(1, half).wait_recv()

        @pl.when(has_above)
        def _(half=half):
            upright(1, half).wait_send()
            upright(0, half).wait_recv()

    @pl.when(has_right)
    def _():
        sideways(0).wait_send()

    @pl.when(has_left)
    def _():
        sideways(1).wait_send()

    lane = lax.broadcasted_iota(jnp.int32, (1, lanes), 1)
    column = jnp.where(lane >= lanes - HALO, lane - lanes, lane) + col_start
    column_ok = jnp.where((column >= 0) & (column < total_cols), 1.0, 0.0)
    for layer in range(layers):
        source, target = layer % 2, 1 - layer % 2

        @pl.loop(0, halves.shape[1] // (4 * unit))
        def _(pair, source=source):
            for one in range(4):
                index = 4 * pair + one
                at = pl.ds(pl.multiple_of(index * unit, unit), unit)
                line = halves[source, at, :]
                wide = line.astype(f32)
                moved = (pltpu.roll(wide, 1, 1).astype(bf16), line, pltpu.roll(wide, lanes - 1, 1).astype(bf16))
                for c in range(3):
                    shifted[pl.ds(pl.multiple_of((3 * index + c) * unit, unit), unit), :] = moved[c]

        left = halo_rows - 2 * layer - 2
        steps = -(-left // BLOCK)

        for index in range(steps):
            start = layer + index * BLOCK
            inside = pl.ds(start * 3 * unit, (BLOCK + 2) * 3 * unit)
            raw = jnp.dot(weight_ref[layer], shifted[inside, :], preferred_element_type=f32)
            hidden = jnp.maximum(raw + bias_ref[layer], 0.0)
            step = lax.broadcasted_iota(jnp.int32, (BLOCK * unit, 1), 0) // unit
            row = step + (start + 1 + row_start)
            row_ok = jnp.where((row >= 0) & (row < total_rows), 1.0, 0.0)
            hidden = (hidden * (row_ok * column_ok)).astype(bf16)
            update = jnp.dot(mixer_ref[layer], hidden, preferred_element_type=f32)
            at = pl.ds((start + 1) * unit, BLOCK * unit)
            halves[target, at, :] = (halves[target, at, :].astype(f32) + update).astype(bf16)

    for half in range(2):
        out_ref[half] = halves[half, HALO * unit:(HALO + rows) * unit, 0:width]


def couple(cells, gradient, inject, kernels, biases, mixers, total_rows, total_cols):
    _, rows, unit, width = cells.shape
    positions = gradient.shape[1]
    half = unit // positions
    layers = kernels.shape[0]
    lanes = -(-(width + 2 * HALO) // 128) * 128
    spaces, coils = lax.axis_size("space"), lax.axis_size("coil")
    held = rows + 2 * HALO + 8
    bias = jnp.tile(biases, (1, positions * BLOCK))[:, :, None]
    spread = jnp.tile(jnp.transpose(inject.reshape(2, half, 2), (0, 2, 1)), (1, 1, positions))[..., None]
    vmem = pl.BlockSpec(memory_space=pltpu.VMEM)
    dma = pltpu.SemaphoreType.DMA
    out = pl.pallas_call(
        functools.partial(couplings_body, layers, rows, width, lanes, total_rows, total_cols, unit, spaces, coils),
        out_shape=jax.ShapeDtypeStruct((2, rows * unit, width), jnp.bfloat16),
        in_specs=[vmem] * 6,
        out_specs=vmem,
        scratch_shapes=[
            pltpu.VMEM((2, held * unit, lanes), jnp.bfloat16),
            pltpu.VMEM((3 * held * unit, lanes), jnp.bfloat16),
            pltpu.VMEM((2, 2, rows * unit, 128), jnp.bfloat16),
            pltpu.VMEM((2, 2, rows * unit, 128), jnp.bfloat16),
            dma((2,)), dma((2,)), dma((2, 2)), dma((2, 2)),
        ],
        compiler_params=pltpu.CompilerParams(
            collective_id=1, has_side_effects=True, vmem_limit_bytes=56 * 1024 * 1024),
    )(cells, gradient, spread, coupling_weights(kernels), mixer_weights(mixers), bias)
    out = out.reshape(2, rows, positions, half, width)
    return jnp.transpose(out, (0, 3, 2, 1, 4)).reshape(2 * half, positions, rows, width)


def per_device(state, sens, kdata, mask, inject, kernels, biases, mixers):
    npar = sens.shape[4]
    npe = kdata.shape[4]
    gradient, cells = find_gradient(state, sens, kdata, mask)
    new_state = couple(cells, gradient, inject, kernels, biases, mixers, npe, npar)
    return (new_state, gradient)


def solution(mesh):
    return jax.shard_map(
        per_device,
        mesh=mesh,
        in_specs=(
            P(None, None, "space", "coil"),
            P(None, "coil", None, "space", None),
            P(None, "coil", None, "space", None),
            P("space", None),
            P(),
            P(),
            P(),
            P(),
        ),
        out_specs=(P(None, None, "space", "coil"), P(None, None, "space", "coil")),
        check_vma=False,
    )
```
